32 devices in a mesh: row: 8 (over z, y), col: 4 (over x, core).
Axes of the slice: x: 2, y: 2, z: 4, core: 2. Of those that a mesh axis runs over, the one named last changes fastest.
Arguments:
- phase: float32 [512, 256, 512], P(None, 'row', 'col'), may hold values from -24 to 24
- pairs: int32 [512, 2], replicated, may hold values from 0 to 127, as said below
Outputs:
- solution: float32 [128, 256, 512], P(None, 'row', 'col')
The draws below stay inside these ranges and needn't reach their ends.
Inputs may be any that keep to these rules, and one draw needn't show every extreme that they name: `pairs`: each row holds two different dates, the earlier one first.
All inputs are finite; a program needn't handle non-finite values.
Results may differ from the reference program's by a relative error of at most 0.00018.
Values sent between devices are 32-bit elements; how exact they have to be, the bound alone decides.
A program may use at most 128 MiB of HBM per device.

```python
import jax
import jax.numpy as jnp
from jax import lax

ND = 128
M = 512
ITERS = 3
NR = 256
NC = 512


def draw_phase(key, part):
    key_base = jax.random.fold_in(key, 11)
    key_rough = jax.random.fold_in(key, 13)
    base = jax.random.normal(key_base, (M, NR, NC), jnp.float32)
    row_pos = jnp.arange(NR, dtype=jnp.float32) / NR
    col_pos = jnp.arange(NC, dtype=jnp.float32) / NC
    rough = jax.random.uniform(key_rough, (NR, NC), jnp.float32, 1.0, 2.0)
    scale = 3.0 ** row_pos[:, None] * 3.0 ** col_pos[None, :] * rough / 3.0
    values = base * scale * 1.5
    return jnp.clip(values, -24.0, 24.0)


def draw_pairs(key, part):
    key_first = jax.random.fold_in(key, 21)
    key_offset = jax.random.fold_in(key, 22)
    first = jax.random.randint(key_first, (M,), 0, ND)
    offset = jax.random.randint(key_offset, (M,), 1, ND)
    second = (first + offset) % ND
    return jnp.stack([jnp.minimum(first, second), jnp.maximum(first, second)], axis=1).astype(jnp.int32)


def setup_inputs(seed: int = 0) -> dict:
    key_list = jax.random.split(jax.random.key(seed), 3)
    return {
        "phase": draw_phase(jax.random.fold_in(key_list[2], 71), 0),
        "pairs": draw_pairs(jax.random.fold_in(key_list[2], 71), 0),
    }


reg_weight = 0.8

def stencil(padded):
    beside = padded[:, 2:, 1:-1] + padded[:, :-2, 1:-1] + padded[:, 1:-1, 2:] + padded[:, 1:-1, :-2]
    return 4.0 * padded[:, 1:-1, 1:-1] - beside

def laplace(field):
    return stencil(jnp.pad(field, ((0, 0), (1, 1), (1, 1))))

def design(pairs):
    dates = jnp.arange(ND, dtype=jnp.int32)
    later = (dates[None, :] == pairs[:, 1:2]).astype(jnp.float32)
    earlier = (dates[None, :] == pairs[:, 0:1]).astype(jnp.float32)
    return later - earlier

def apply_design(matrix, field):
    flat = field.reshape(field.shape[0], -1)
    result = jnp.dot(matrix, flat, precision=lax.Precision.HIGHEST, preferred_element_type=jnp.float32)
    return result.reshape((matrix.shape[0],) + field.shape[1:])

def reference(phase, pairs):
    matrix = design(pairs)
    transpose = matrix.T
    beta_norm = jnp.sqrt(jnp.sum(phase * phase))
    left_data = phase / beta_norm
    pulled = apply_design(transpose, left_data)
    alpha_norm = jnp.sqrt(jnp.sum(pulled * pulled))
    right_vec = pulled / alpha_norm
    left_reg = jnp.zeros((ND, NR, NC), jnp.float32)
    search_dir = right_vec
    solution = jnp.zeros_like(right_vec)
    phi_bar = beta_norm
    rho_bar = alpha_norm
    for step in range(ITERS):
        fwd_data = apply_design(matrix, right_vec) - alpha_norm * left_data
        fwd_reg = reg_weight * laplace(right_vec) - alpha_norm * left_reg
        beta_norm = jnp.sqrt(jnp.sum(fwd_data * fwd_data) + jnp.sum(fwd_reg * fwd_reg))
        left_data = fwd_data / beta_norm
        left_reg = fwd_reg / beta_norm
        pulled = apply_design(transpose, left_data) + reg_weight * laplace(left_reg) - beta_norm * right_vec
        alpha_norm = jnp.sqrt(jnp.sum(pulled * pulled))
        right_vec = pulled / alpha_norm
        rho_new = jnp.sqrt(rho_bar * rho_bar + beta_norm * beta_norm)
        cosine = rho_bar / rho_new
        sine_val = beta_norm / rho_new
        theta_val = sine_val * alpha_norm
        rho_bar = -cosine * alpha_norm
        phi_new = cosine * phi_bar
        phi_bar = sine_val * phi_bar
        solution = solution + phi_new / rho_new * search_dir
        search_dir = right_vec - theta_val / rho_new * search_dir
    return solution
```

```python
import functools

import jax
import jax.numpy as jnp
from jax import lax
from jax.experimental import pallas as pl
from jax.experimental.pallas import tpu as pltpu
from jax.sharding import PartitionSpec as P

ND = 128
ITERS = 3
LAM = 0.8

MESH = pl.DeviceIdType.MESH
STEPS = ((-1, 0), (1, 0), (0, -1), (0, 1), (1, 1), (1, -1), (-1, 1), (-1, -1))


def split(x):
    high = x.astype(jnp.bfloat16)
    return high, (x - high.astype(jnp.float32)).astype(jnp.bfloat16)


def folded(x):
    return jnp.sum(x.reshape(x.shape[0] // 8, 8, x.shape[1]), axis=0)


def inverse(x):
    return jnp.where(x > 0.0, 1.0 / x, 0.0)


def coefficients(mu, beta, shift, scale):
    def inner(p, q, off=0):
        total = 0.0
        for i, a in enumerate(p):
            for j, b in enumerate(q):
                total = total + a * b * mu[i + j + off]
        return total

    zero = jnp.zeros_like(beta)
    alpha = jnp.sqrt(mu[0]) / beta
    vec = [1.0 / (alpha * beta)]
    before, coupling, theta = [zero], zero, zero
    search, phi_bar, total = [zero], beta, [zero] * ITERS
    rho, phi = None, None
    for step in range(ITERS):
        mean = inner(vec, vec, 1)
        rho_sq = scale * mean + shift * inner(vec, vec) - theta * theta
        inv_rho = inverse(jnp.sqrt(jnp.maximum(rho_sq, 0.0)))
        if step == 0:
            phi = alpha * phi_bar * inv_rho
            search = vec
        else:
            phi = -theta * phi * inv_rho
            past = search + [zero] * (len(vec) - len(search))
            search = [a - theta * inv_before * b for a, b in zip(vec, past)]
        for i, a in enumerate(search):
            total[i] = total[i] + phi * inv_rho * a
        if step < ITERS - 1:
            up = [zero] + vec
            mid = vec + [zero]
            low = before + [zero] * (len(up) - len(before))
            nxt = [a - mean * b - coupling * c for a, b, c in zip(up, mid, low)]
            coupling = jnp.sqrt(jnp.maximum(inner(nxt, nxt), 0.0))
            before = vec
            vec = [a * inverse(coupling) for a in nxt]
            theta = scale * coupling * inv_rho
            inv_before = inv_rho
    return total


def kernel(dims, phase, pairs, out, held, v0, v1, v2, side, side_t, from_left, from_right,
           corner, beside, temp, acc, mine, cols_in, part, rows_in, load_sem, send_sem, recv_sem,
           col_send, col_recv, row_send, row_recv):
    n_row, n_col, count, rows, cols = dims
    tiles, pairs_of_rows = rows // 8, rows // 2
    vecs = (v0, v1, v2)
    row, col = lax.axis_index("row"), lax.axis_index("col")

    loads = [
        pltpu.make_async_copy(phase.at[:, t], held.at[t], load_sem.at[t]) for t in range(tiles)
    ]
    order = [0, tiles - 1] + list(range(1, tiles - 1))
    for t in order:
        loads[t].start()

    def exists(dr, dc):
        ok = None
        for pos, step, n in ((row, dr, n_row), (col, dc, n_col)):
            if step:
                here = pos + step >= 0 if step < 0 else pos + step < n
                ok = here if ok is None else jnp.logical_and(ok, here)
        return ok

    barrier = pltpu.get_barrier_semaphore()
    for d in range(1, n_row):
        pl.semaphore_signal(
            barrier, inc=1, device_id=(lax.rem(row + d, n_row), col), device_id_type=MESH
        )
    for d in range(1, n_col):
        pl.semaphore_signal(
            barrier, inc=1, device_id=(row, lax.rem(col + d, n_col)), device_id_type=MESH
        )
    for dr, dc in STEPS[4:]:
        @pl.when(exists(dr, dc))
        def _():
            pl.semaphore_signal(
                barrier, inc=1, device_id=(row + dr, col + dc), device_id_type=MESH
            )

    def beside_count(pos, n):
        return jnp.where(pos > 0, 1, 0) + jnp.where(pos < n - 1, 1, 0)

    def meet():
        corners = beside_count(row, n_row) * beside_count(col, n_col)
        pl.semaphore_wait(barrier, n_row + n_col - 2 + corners)

    def message(k, i, receiving=False):
        dr, dc = STEPS[i]
        v = vecs[k]
        low, high = side_t.at[k, pl.ds(0, 8)], side_t.at[k, pl.ds(4 * rows - 8, 8)]
        src, dst = (
            (v.at[pl.ds(2, 2)], v.at[pl.ds(rows + 2, 2)]),
            (v.at[pl.ds(rows, 2)], v.at[pl.ds(0, 2)]),
            (side.at[k], from_right.at[k]),
            (side.at[k], from_left.at[k]),
            (high, corner.at[k, 0]),
            (high, corner.at[k, 1]),
            (low, corner.at[k, 2]),
            (low, corner.at[k, 3]),
        )[i]
        sign = -1 if receiving else 1
        return pltpu.make_async_remote_copy(
            src_ref=src, dst_ref=dst, send_sem=send_sem.at[k, i], recv_sem=recv_sem.at[k, i],
            device_id=(row + sign * dr, col + sign * dc), device_id_type=MESH,
        )

    def send(k, which):
        for i in which:
            @pl.when(exists(*STEPS[i]))
            def _():
                message(k, i).start()

    def receive(k, which):
        for i in which:
            dr, dc = STEPS[i]
            @pl.when(exists(-dr, -dc))
            def _():
                message(k, i, True).wait_recv()

    for i, (dr, dc) in enumerate(STEPS):
        @pl.when(jnp.logical_not(exists(-dr, -dc)))
        def _():
            for k in range(ITERS):
                if i == 0:
                    vecs[k][pl.ds(rows + 2, 2)] = jnp.zeros((2, ND, cols), jnp.float32)
                elif i == 1:
                    vecs[k][pl.ds(0, 2)] = jnp.zeros((2, ND, cols), jnp.float32)
                elif i == 2:
                    from_right[k] = jnp.zeros((ND, cols), jnp.float32)
                elif i == 3:
                    from_left[k] = jnp.zeros((ND, cols), jnp.float32)
                else:
                    corner[k, i - 4] = jnp.zeros((8, ND), jnp.float32)

    acc[...] = jnp.zeros_like(acc)
    lane = lax.broadcasted_iota(jnp.int32, (ND, cols), 1)

    dates = lax.broadcasted_iota(jnp.int32, (count, ND), 1)
    design = (dates == pairs[:, 1:2]).astype(jnp.float32) - (dates == pairs[:, 0:1]).astype(
        jnp.float32
    )
    pull = design.T.astype(jnp.bfloat16)
    gram = jnp.dot(pull, design.astype(jnp.bfloat16), preferred_element_type=jnp.float32)
    gram_high, gram_low = split(gram)
    normal = jnp.concatenate(
        [
            jnp.concatenate([gram_high, gram_high], axis=1),
            jnp.concatenate([gram_low, gram_low], axis=1),
        ],
        axis=0,
    )

    shift = 2.0 * count / ND + 20.0 * LAM * LAM
    scale = 0.75 * shift
    k2 = LAM * LAM / scale

    def put(k, r, x):
        vecs[k][r + 2] = x
        side[k] = jnp.where(lane // 4 == r, pltpu.roll(x, 4 * r + 2, 1), side[k])

    def pulled(t, p):
        flat = held.at[t].reshape(count * 8, cols)
        x = jnp.concatenate(
            [flat[pl.ds(2 * p + j, count, stride=8), :] for j in range(2)], axis=1
        )
        square = x * x
        acc[6] += folded(square[:, :cols] + square[:, cols:])
        high, low = split(x)
        b = jnp.dot(pull, high, preferred_element_type=jnp.float32) + jnp.dot(
            pull, low, preferred_element_type=jnp.float32
        )
        r = 8 * t + 2 * p
        put(0, r, b[:, :cols])
        put(0, r + 1, b[:, cols:])

    side[0] = jnp.zeros((ND, cols), jnp.float32)
    for n, t in enumerate(order):
        loads[t].wait()

        @pl.loop(0, 4)
        def _(p):
            pulled(t, p)

        if n == min(1, tiles - 1):
            meet()
            send(0, (0, 1))

    def finish_sides(k):
        send(k, (2, 3))
        side_t[k] = side[k].T
        send(k, (4, 5, 6, 7))

    finish_sides(0)

    sub = lax.broadcasted_iota(jnp.int32, (cols, ND), 0)
    col_out = jnp.where(jnp.logical_and(lane == 0, col == 0), 1.0, 0.0) + jnp.where(
        jnp.logical_and(lane == cols - 1, col == n_col - 1), 1.0, 0.0
    )

    def horizontal(x, y):
        return pltpu.roll(jnp.where(lane == cols - 1, y, x), 1, 1) + pltpu.roll(
            jnp.where(lane == 0, y, x), cols - 1, 1
        )

    for k in range(ITERS):
        v = vecs[k]
        last = k == ITERS - 1

        @pl.loop(0, pairs_of_rows)
        def _(p):
            r = 2 * p
            x = jnp.concatenate([v[r + 2], v[r + 3]], axis=1)
            both = jnp.concatenate(split(x), axis=0)
            y = jnp.dot(normal, both, preferred_element_type=jnp.float32)
            y = (y[:ND] + y[ND:]) * (1.0 / scale)
            temp[r] = y[:, :cols]
            temp[r + 1] = y[:, cols:]

        receive(k, (2, 3))
        side_in = jnp.where(lax.rem(lane, 4) < 2, from_left[k], from_right[k])
        from_left[k] = side_in

        @pl.loop(0, rows)
        def _(r):
            x = v[r + 2]
            y = pltpu.roll(from_left[k], lax.rem(2 * cols - 2 - 4 * r, cols), 1)
            h = horizontal(x, y)
            d2 = pltpu.roll(jnp.where(lane >= cols - 2, y, x), 2, 1) + pltpu.roll(
                jnp.where(lane < 2, y, x), cols - 2, 1
            )
            edge = jnp.where(jnp.logical_and(r == 0, row == 0), 1.0, 0.0) + jnp.where(
                jnp.logical_and(r == rows - 1, row == n_row - 1), 1.0, 0.0
            )
            centre = (20.0 * k2 - shift / scale) - k2 * (col_out + edge)
            beside[r + 1] = h
            temp[r] = temp[r] + centre * x + k2 * (d2 - 8.0 * h)

        receive(k, (0, 1, 4, 5, 6, 7))
        for at, h_at, left, right, a, b in (
            (1, 0, 0, 1, 5, 6),
            (rows + 2, rows + 1, 2, 3, 1, 2),
        ):
            m = jnp.where(
                sub == cols - 1,
                corner[k, left, pl.ds(a, 1), :],
                jnp.where(sub == 0, corner[k, right, pl.ds(b, 1), :], 0.0),
            )
            beside[h_at] = horizontal(v[at], m.T)

        if not last:
            side[k + 1] = jnp.zeros((ND, cols), jnp.float32)

        def both_rows(p):
            r = 2 * p
            x = [v[r + j] for j in range(6)]
            h = [beside[r + j] for j in range(4)]
            new = [
                temp[r + j]
                + k2 * (2.0 * (h[j] + h[j + 2]) + (x[j] + x[j + 4]) - 8.0 * (x[j + 1] + x[j + 3]))
                for j in range(2)
            ]
            if k == 0:
                acc[0] += folded(x[2] * x[2] + x[3] * x[3])
            acc[2 * k + 1] += folded(x[2] * new[0] + x[3] * new[1])
            if not last:
                acc[2 * k + 2] += folded(new[0] * new[0] + new[1] * new[1])
                put(k + 1, r, new[0])
                put(k + 1, r + 1, new[1])

        @pl.loop(0, 2)
        def _(e):
            both_rows(e * (pairs_of_rows - 1))

        if not last:
            send(k + 1, (0, 1))

        @pl.loop(1, pairs_of_rows - 1)
        def _(p):
            both_rows(p)

        if not last:
            finish_sides(k + 1)

    slot = lax.broadcasted_iota(jnp.int32, (8, cols), 0)
    local = jnp.zeros((8, cols), jnp.float32)
    for j in range(7):
        local = jnp.where(slot == j, jnp.sum(acc[j], axis=0, keepdims=True), local)

    def gather(source, into, send_s, recv_s, me, n, where_to):
        into[me] = source[...]
        copies = []
        for d in range(1, n):
            c = pltpu.make_async_remote_copy(
                src_ref=source, dst_ref=into.at[n + d], send_sem=send_s.at[d],
                recv_sem=recv_s.at[d], device_id=where_to(lax.rem(me + d, n)),
                device_id_type=MESH,
            )
            c.start()
            copies.append(c)
        for d, c in enumerate(copies, 1):
            c.wait()
            into[lax.rem(me + n - d, n)] = into[n + d]
        total = into[0]
        for i in range(1, n):
            total = total + into[i]
        return total

    mine[...] = local
    part[...] = gather(mine, cols_in, col_send, col_recv, col, n_col, lambda c: (row, c))
    sums = gather(part, rows_in, row_send, row_recv, row, n_row, lambda r: (r, col))
    sums = jnp.broadcast_to(jnp.sum(sums, axis=1, keepdims=True), (8, cols))
    mu = [sums[j : j + 1] for j in range(6)]
    y = coefficients(mu, jnp.sqrt(sums[6:7]), shift, scale)

    @pl.loop(0, rows)
    def _(r):
        out[pl.ds(r, ND, stride=rows), :] = y[0] * v0[r + 2] + y[1] * v1[r + 2] + y[2] * v2[r + 2]

    for k in range(ITERS):
        for i, step in enumerate(STEPS):
            @pl.when(exists(*step))
            def _():
                message(k, i).wait_send()


def on_device(n_row, n_col, phase, pairs):
    count, rows, cols = phase.shape
    assert rows % 8 == 0 and 4 * rows == cols and cols == ND
    f32 = jnp.float32
    dma = pltpu.SemaphoreType.DMA
    result = pl.pallas_call(
        functools.partial(kernel, (n_row, n_col, count, rows, cols)),
        out_shape=jax.ShapeDtypeStruct((ND * rows, cols), f32),
        in_specs=[pl.BlockSpec(memory_space=pl.ANY), pl.BlockSpec(memory_space=pltpu.VMEM)],
        out_specs=pl.BlockSpec(memory_space=pltpu.VMEM),
        scratch_shapes=[
            pltpu.VMEM((rows // 8, count, 8, cols), f32),
            pltpu.VMEM((rows + 4, ND, cols), f32),
            pltpu.VMEM((rows + 4, ND, cols), f32),
            pltpu.VMEM((rows + 4, ND, cols), f32),
            pltpu.VMEM((ITERS, ND, cols), f32),
            pltpu.VMEM((ITERS, cols, ND), f32),
            pltpu.VMEM((ITERS, ND, cols), f32),
            pltpu.VMEM((ITERS, ND, cols), f32),
            pltpu.VMEM((ITERS, 4, 8, ND), f32),
            pltpu.VMEM((rows + 2, ND, cols), f32),
            pltpu.VMEM((rows, ND, cols), f32),
            pltpu.VMEM((8, 8, cols), f32),
            pltpu.VMEM((8, cols), f32),
            pltpu.VMEM((2 * n_col, 8, cols), f32),
            pltpu.VMEM((8, cols), f32),
            pltpu.VMEM((2 * n_row, 8, cols), f32),
            dma((rows // 8,)),
            dma((ITERS, 8)),
            dma((ITERS, 8)),
            dma((n_col,)),
            dma((n_col,)),
            dma((n_row,)),
            dma((n_row,)),
        ],
        compiler_params=pltpu.CompilerParams(
            collective_id=0, has_side_effects=True, vmem_limit_bytes=48 * 1024 * 1024
        ),
    )(phase.reshape(count, rows // 8, 8, cols), pairs)
    return result.reshape(ND, rows, cols)


def solution(mesh):
    shape = mesh.shape
    return jax.shard_map(
        functools.partial(on_device, shape["row"], shape["col"]),
        mesh=mesh,
        in_specs=(P(None, "row", "col"), P()),
        out_specs=P(None, "row", "col"),
        check_vma=False,
    )
```

```python
import functools

import jax
import jax.numpy as jnp
from jax import lax
from jax.experimental import pallas as pl
from jax.experimental.pallas import tpu as pltpu
from jax.sharding import PartitionSpec as P

ND = 128
ITERS = 3
LAM = 0.8

MESH = pl.DeviceIdType.MESH
STEPS = ((-1, 0), (1, 0), (0, -1), (0, 1), (1, 1), (1, -1), (-1, 1), (-1, -1))


def split(x):
    high = x.astype(jnp.bfloat16)
    return high, (x - high.astype(jnp.float32)).astype(jnp.bfloat16)


def folded(x):
    return jnp.sum(x.reshape(x.shape[0] // 8, 8, x.shape[1]), axis=0)


def inverse(x):
    return jnp.where(x > 0.0, 1.0 / x, 0.0)


def coefficients(mu, beta, shift, scale):
    def inner(p, q, off=0):
        total = 0.0
        for i, a in enumerate(p):
            for j, b in enumerate(q):
                total = total + a * b * mu[i + j + off]
        return total

    zero = jnp.zeros_like(beta)
    alpha = jnp.sqrt(mu[0]) / beta
    vec = [1.0 / (alpha * beta)]
    before, coupling, theta = [zero], zero, zero
    search, phi_bar, total = [zero], beta, [zero] * ITERS
    rho, phi = None, None
    for step in range(ITERS):
        mean = inner(vec, vec, 1)
        rho_sq = scale * mean + shift * inner(vec, vec) - theta * theta
        inv_rho = inverse(jnp.sqrt(jnp.maximum(rho_sq, 0.0)))
        if step == 0:
            phi = alpha * phi_bar * inv_rho
            search = vec
        else:
            phi = -theta * phi * inv_rho
            past = search + [zero] * (len(vec) - len(search))
            search = [a - theta * inv_before * b for a, b in zip(vec, past)]
        for i, a in enumerate(search):
            total[i] = total[i] + phi * inv_rho * a
        if step < ITERS - 1:
            up = [zero] + vec
            mid = vec + [zero]
            low = before + [zero] * (len(up) - len(before))
            nxt = [a - mean * b - coupling * c for a, b, c in zip(up, mid, low)]
            coupling = jnp.sqrt(jnp.maximum(inner(nxt, nxt), 0.0))
            before = vec
            vec = [a * inverse(coupling) for a in nxt]
            theta = scale * coupling * inv_rho
            inv_before = inv_rho
    return total


def kernel(dims, phase, pairs, out, held, v0, v1, v2, side, side_t, from_left, from_right,
           corner, beside, temp, acc, mine, cols_in, part, rows_in, load_sem, send_sem, recv_sem,
           col_send, col_recv, row_send, row_recv):
    n_row, n_col, count, rows, cols = dims
    tiles, pairs_of_rows = rows // 8, rows // 2
    vecs = (v0, v1, v2)
    row, col = lax.axis_index("row"), lax.axis_index("col")

    loads = [
        pltpu.make_async_copy(phase.at[:, t], held.at[t], load_sem.at[t]) for t in range(tiles)
    ]
    order = [0, tiles - 1] + list(range(1, tiles - 1))
    for t in order:
        loads[t].start()

    def exists(dr, dc):
        ok = None
        for pos, step, n in ((row, dr, n_row), (col, dc, n_col)):
            if step:
                here = pos + step >= 0 if step < 0 else pos + step < n
                ok = here if ok is None else jnp.logical_and(ok, here)
        return ok

    barrier = pltpu.get_barrier_semaphore()
    for d in range(1, n_row):
        pl.semaphore_signal(
            barrier, inc=1, device_id=(lax.rem(row + d, n_row), col), device_id_type=MESH
        )
    for d in range(1, n_col):
        pl.semaphore_signal(
            barrier, inc=1, device_id=(row, lax.rem(col + d, n_col)), device_id_type=MESH
        )
    for dr, dc in STEPS[4:]:
        @pl.when(exists(dr, dc))
        def _():
            pl.semaphore_signal(
                barrier, inc=1, device_id=(row + dr, col + dc), device_id_type=MESH
            )

    def beside_count(pos, n):
        return jnp.where(pos > 0, 1, 0) + jnp.where(pos < n - 1, 1, 0)

    def meet():
        corners = beside_count(row, n_row) * beside_count(col, n_col)
        pl.semaphore_wait(barrier, n_row + n_col - 2 + corners)

    def message(k, i, receiving=False):
        dr, dc = STEPS[i]
        v = vecs[k]
        low, high = side_t.at[k, pl.ds(0, 8)], side_t.at[k, pl.ds(4 * rows - 8, 8)]
        src, dst = (
            (v.at[pl.ds(2, 2)], v.at[pl.ds(rows + 2, 2)]),
            (v.at[pl.ds(rows, 2)], v.at[pl.ds(0, 2)]),
            (side.at[k], from_right.at[k]),
            (side.at[k], from_left.at[k]),
            (high, corner.at[k, 0]),
            (high, corner.at[k, 1]),
            (low, corner.at[k, 2]),
            (low, corner.at[k, 3]),
        )[i]
        sign = -1 if receiving else 1
        return pltpu.make_async_remote_copy(
            src_ref=src, dst_ref=dst, send_sem=send_sem.at[k, i], recv_sem=recv_sem.at[k, i],
            device_id=(row + sign * dr, col + sign * dc), device_id_type=MESH,
        )

    def send(k, which):
        for i in which:
            @pl.when(exists(*STEPS[i]))
            def _():
                message(k, i).start()

    def receive(k, which):
        for i in which:
            dr, dc = STEPS[i]
            @pl.when(exists(-dr, -dc))
            def _():
                message(k, i, True).wait_recv()

    for i, (dr, dc) in enumerate(STEPS):
        @pl.when(jnp.logical_not(exists(-dr, -dc)))
        def _():
            for k in range(ITERS):
                if i == 0:
                    vecs[k][pl.ds(rows + 2, 2)] = jnp.zeros((2, ND, cols), jnp.float32)
                elif i == 1:
                    vecs[k][pl.ds(0, 2)] = jnp.zeros((2, ND, cols), jnp.float32)
                elif i == 2:
                    from_right[k] = jnp.zeros((ND, cols), jnp.float32)
                elif i == 3:
                    from_left[k] = jnp.zeros((ND, cols), jnp.float32)
                else:
                    corner[k, i - 4] = jnp.zeros((8, ND), jnp.float32)

    acc[...] = jnp.zeros_like(acc)
    lane = lax.broadcasted_iota(jnp.int32, (ND, cols), 1)

    dates = lax.broadcasted_iota(jnp.int32, (ND, count), 0)
    pull = (dates == pairs[1:2, :]).astype(jnp.float32) - (dates == pairs[0:1, :]).astype(
        jnp.float32
    )
    pull = pull.astype(jnp.bfloat16)
    gram = lax.dot_general(
        pull, pull, (((1,), (1,)), ((), ())), preferred_element_type=jnp.float32
    )
    gram_high, gram_low = split(gram)
    normal = jnp.concatenate(
        [
            jnp.concatenate([gram_high, gram_high], axis=1),
            jnp.concatenate([gram_low, gram_low], axis=1),
        ],
        axis=0,
    )

    shift = 2.0 * count / ND + 20.0 * LAM * LAM
    scale = 0.75 * shift
    k2 = LAM * LAM / scale

    def put(k, r, x):
        vecs[k][r + 2] = x
        side[k] = jnp.where(lane // 4 == r, pltpu.roll(x, 4 * r + 2, 1), side[k])

    def pulled(t, p):
        flat = held.at[t].reshape(count * 8, cols)
        x = jnp.concatenate(
            [flat[pl.ds(2 * p + j, count, stride=8), :] for j in range(2)], axis=1
        )
        square = x * x
        acc[6] += folded(square[:, :cols] + square[:, cols:])
        high, low = split(x)
        b = jnp.dot(pull, high, preferred_element_type=jnp.float32) + jnp.dot(
            pull, low, preferred_element_type=jnp.float32
        )
        r = 8 * t + 2 * p
        put(0, r, b[:, :cols])
        put(0, r + 1, b[:, cols:])

    side[0] = jnp.zeros((ND, cols), jnp.float32)
    for n, t in enumerate(order):
        loads[t].wait()

        @pl.loop(0, 4)
        def _(p):
            pulled(t, p)

        if n == min(1, tiles - 1):
            meet()
            send(0, (0, 1))

    def finish_sides(k):
        send(k, (2, 3))
        side_t[k] = side[k].T
        send(k, (4, 5, 6, 7))

    finish_sides(0)

    sub = lax.broadcasted_iota(jnp.int32, (cols, ND), 0)
    col_out = jnp.where(jnp.logical_and(lane == 0, col == 0), 1.0, 0.0) + jnp.where(
        jnp.logical_and(lane == cols - 1, col == n_col - 1), 1.0, 0.0
    )

    def horizontal(x, y):
        return pltpu.roll(jnp.where(lane == cols - 1, y, x), 1, 1) + pltpu.roll(
            jnp.where(lane == 0, y, x), cols - 1, 1
        )

    for k in range(ITERS):
        v = vecs[k]
        last = k == ITERS - 1

        @pl.loop(0, pairs_of_rows, unroll=4)
        def _(p):
            r = 2 * p
            x = jnp.concatenate([v[r + 2], v[r + 3]], axis=1)
            both = jnp.concatenate(split(x), axis=0)
            y = jnp.dot(normal, both, preferred_element_type=jnp.float32)
            y = (y[:ND] + y[ND:]) * (1.0 / scale)
            temp[r] = y[:, :cols]
            temp[r + 1] = y[:, cols:]

        receive(k, (2, 3))
        side_in = jnp.where(lax.rem(lane, 4) < 2, from_left[k], from_right[k])
        from_left[k] = side_in

        @pl.loop(0, rows, unroll=4)
        def _(r):
            x = v[r + 2]
            y = pltpu.roll(from_left[k], lax.rem(2 * cols - 2 - 4 * r, cols), 1)
            h = horizontal(x, y)
            d2 = pltpu.roll(jnp.where(lane >= cols - 2, y, x), 2, 1) + pltpu.roll(
                jnp.where(lane < 2, y, x), cols - 2, 1
            )
            edge = jnp.where(jnp.logical_and(r == 0, row == 0), 1.0, 0.0) + jnp.where(
                jnp.logical_and(r == rows - 1, row == n_row - 1), 1.0, 0.0
            )
            centre = (20.0 * k2 - shift / scale) - k2 * (col_out + edge)
            beside[r + 1] = h
            temp[r] = temp[r] + centre * x + k2 * (d2 - 8.0 * h)

        receive(k, (0, 1, 4, 5, 6, 7))
        for at, h_at, left, right, a, b in (
            (1, 0, 0, 1, 5, 6),
            (rows + 2, rows + 1, 2, 3, 1, 2),
        ):
            m = jnp.where(
                sub == cols - 1,
                corner[k, left, pl.ds(a, 1), :],
                jnp.where(sub == 0, corner[k, right, pl.ds(b, 1), :], 0.0),
            )
            beside[h_at] = horizontal(v[at], m.T)

        if not last:
            side[k + 1] = jnp.zeros((ND, cols), jnp.float32)

        def both_rows(p):
            r = 2 * p
            x = [v[r + j] for j in range(6)]
            h = [beside[r + j] for j in range(4)]
            new = [
                temp[r + j]
                + k2 * (2.0 * (h[j] + h[j + 2]) + (x[j] + x[j + 4]) - 8.0 * (x[j + 1] + x[j + 3]))
                for j in range(2)
            ]
            if k == 0:
                acc[0] += folded(x[2] * x[2] + x[3] * x[3])
            acc[2 * k + 1] += folded(x[2] * new[0] + x[3] * new[1])
            if not last:
                acc[2 * k + 2] += folded(new[0] * new[0] + new[1] * new[1])
                put(k + 1, r, new[0])
                put(k + 1, r + 1, new[1])

        @pl.loop(0, 2)
        def _(e):
            both_rows(e * (pairs_of_rows - 1))

        if not last:
            send(k + 1, (0, 1))

        @pl.loop(1, pairs_of_rows - 1, unroll=2)
        def _(p):
            both_rows(p)

        if not last:
            finish_sides(k + 1)

    slot = lax.broadcasted_iota(jnp.int32, (8, cols), 0)
    local = jnp.zeros((8, cols), jnp.float32)
    for j in range(7):
        local = jnp.where(slot == j, jnp.sum(acc[j], axis=0, keepdims=True), local)

    def gather(source, into, send_s, recv_s, me, n, where_to):
        into[me] = source[...]
        copies = []
        for d in range(1, n):
            c = pltpu.make_async_remote_copy(
                src_ref=source, dst_ref=into.at[n + d], send_sem=send_s.at[d],
                recv_sem=recv_s.at[d], device_id=where_to(lax.rem(me + d, n)),
                device_id_type=MESH,
            )
            c.start()
            copies.append(c)
        for d, c in enumerate(copies, 1):
            c.wait()
            into[lax.rem(me + n - d, n)] = into[n + d]
        total = into[0]
        for i in range(1, n):
            total = total + into[i]
        return total

    mine[...] = local
    part[...] = gather(mine, cols_in, col_send, col_recv, col, n_col, lambda c: (row, c))
    sums = gather(part, rows_in, row_send, row_recv, row, n_row, lambda r: (r, col))
    sums = jnp.broadcast_to(jnp.sum(sums, axis=1, keepdims=True), (8, cols))
    mu = [sums[j : j + 1] for j in range(6)]
    y = coefficients(mu, jnp.sqrt(sums[6:7]), shift, scale)

    @pl.loop(0, rows, unroll=4)
    def _(r):
        out[pl.ds(r, ND, stride=rows), :] = y[0] * v0[r + 2] + y[1] * v1[r + 2] + y[2] * v2[r + 2]

    for k in range(ITERS):
        for i, step in enumerate(STEPS):
            @pl.when(exists(*step))
            def _():
                message(k, i).wait_send()


def on_device(n_row, n_col, phase, pairs):
    count, rows, cols = phase.shape
    assert rows % 8 == 0 and 4 * rows == cols and cols == ND
    f32 = jnp.float32
    dma = pltpu.SemaphoreType.DMA
    result = pl.pallas_call(
        functools.partial(kernel, (n_row, n_col, count, rows, cols)),
        out_shape=jax.ShapeDtypeStruct((ND * rows, cols), f32),
        in_specs=[pl.BlockSpec(memory_space=pl.ANY), pl.BlockSpec(memory_space=pltpu.VMEM)],
        out_specs=pl.BlockSpec(memory_space=pltpu.VMEM),
        scratch_shapes=[
            pltpu.VMEM((rows // 8, count, 8, cols), f32),
            pltpu.VMEM((rows + 4, ND, cols), f32),
            pltpu.VMEM((rows + 4, ND, cols), f32),
            pltpu.VMEM((rows + 4, ND, cols), f32),
            pltpu.VMEM((ITERS, ND, cols), f32),
            pltpu.VMEM((ITERS, cols, ND), f32),
            pltpu.VMEM((ITERS, ND, cols), f32),
            pltpu.VMEM((ITERS, ND, cols), f32),
            pltpu.VMEM((ITERS, 4, 8, ND), f32),
            pltpu.VMEM((rows + 2, ND, cols), f32),
            pltpu.VMEM((rows, ND, cols), f32),
            pltpu.VMEM((8, 8, cols), f32),
            pltpu.VMEM((8, cols), f32),
            pltpu.VMEM((2 * n_col, 8, cols), f32),
            pltpu.VMEM((8, cols), f32),
            pltpu.VMEM((2 * n_row, 8, cols), f32),
            dma((rows // 8,)),
            dma((ITERS, 8)),
            dma((ITERS, 8)),
            dma((n_col,)),
            dma((n_col,)),
            dma((n_row,)),
            dma((n_row,)),
        ],
        compiler_params=pltpu.CompilerParams(
            collective_id=0, has_side_effects=True, vmem_limit_bytes=48 * 1024 * 1024
        ),
    )(phase.reshape(count, rows // 8, 8, cols), pairs.T)
    return result.reshape(ND, rows, cols)


def solution(mesh):
    shape = mesh.shape
    return jax.shard_map(
        functools.partial(on_device, shape["row"], shape["col"]),
        mesh=mesh,
        in_specs=(P(None, "row", "col"), P()),
        out_specs=P(None, "row", "col"),
        check_vma=False,
    )
```

```python
import functools

import jax
import jax.numpy as jnp
from jax import lax
from jax.experimental import pallas as pl
from jax.experimental.pallas import tpu as pltpu
from jax.sharding import PartitionSpec as P

ND = 128
ITERS = 3
LAM = 0.8

MESH = pl.DeviceIdType.MESH
STEPS = ((-1, 0), (1, 0), (0, -1), (0, 1), (1, 1), (1, -1), (-1, 1), (-1, -1))


def split(x):
    high = x.astype(jnp.bfloat16)
    return high, (x - high.astype(jnp.float32)).astype(jnp.bfloat16)


def folded(x):
    return jnp.sum(x.reshape(x.shape[0] // 8, 8, x.shape[1]), axis=0)


def inverse(x):
    return jnp.where(x > 0.0, 1.0 / x, 0.0)


def coefficients(mu, beta, shift, scale):
    def inner(p, q, off=0):
        total = 0.0
        for i, a in enumerate(p):
            for j, b in enumerate(q):
                total = total + a * b * mu[i + j + off]
        return total

    zero = jnp.zeros_like(beta)
    alpha = jnp.sqrt(mu[0]) / beta
    vec = [1.0 / (alpha * beta)]
    before, coupling, theta = [zero], zero, zero
    search, phi_bar, total = [zero], beta, [zero] * ITERS
    rho, phi = None, None
    for step in range(ITERS):
        mean = inner(vec, vec, 1)
        rho_sq = scale * mean + shift * inner(vec, vec) - theta * theta
        inv_rho = inverse(jnp.sqrt(jnp.maximum(rho_sq, 0.0)))
        if step == 0:
            phi = alpha * phi_bar * inv_rho
            search = vec
        else:
            phi = -theta * phi * inv_rho
            past = search + [zero] * (len(vec) - len(search))
            search = [a - theta * inv_before * b for a, b in zip(vec, past)]
        for i, a in enumerate(search):
            total[i] = total[i] + phi * inv_rho * a
        if step < ITERS - 1:
            up = [zero] + vec
            mid = vec + [zero]
            low = before + [zero] * (len(up) - len(before))
            nxt = [a - mean * b - coupling * c for a, b, c in zip(up, mid, low)]
            coupling = jnp.sqrt(jnp.maximum(inner(nxt, nxt), 0.0))
            before = vec
            vec = [a * inverse(coupling) for a in nxt]
            theta = scale * coupling * inv_rho
            inv_before = inv_rho
    return total


def kernel(dims, phase, pairs, out, held, v0, v1, v2, side, side_t, from_left, from_right,
           corner, beside, temp, acc, mine, cols_in, part, rows_in, load_sem, send_sem, recv_sem,
           col_send, col_recv, row_send, row_recv):
    n_row, n_col, count, rows, cols = dims
    tiles, pairs_of_rows = rows // 8, rows // 2
    vecs = (v0, v1, v2)
    row, col = lax.axis_index("row"), lax.axis_index("col")

    loads = [
        pltpu.make_async_copy(phase.at[:, t], held.at[t], load_sem.at[t]) for t in range(tiles)
    ]
    order = [0, tiles - 1] + list(range(1, tiles - 1))
    for t in order:
        loads[t].start()

    def exists(dr, dc):
        ok = None
        for pos, step, n in ((row, dr, n_row), (col, dc, n_col)):
            if step:
                here = pos + step >= 0 if step < 0 else pos + step < n
                ok = here if ok is None else jnp.logical_and(ok, here)
        return ok

    barrier = pltpu.get_barrier_semaphore()
    for d in range(1, n_row):
        pl.semaphore_signal(
            barrier, inc=1, device_id=(lax.rem(row + d, n_row), col), device_id_type=MESH
        )
    for d in range(1, n_col):
        pl.semaphore_signal(
            barrier, inc=1, device_id=(row, lax.rem(col + d, n_col)), device_id_type=MESH
        )
    for dr, dc in STEPS[4:]:
        @pl.when(exists(dr, dc))
        def _():
            pl.semaphore_signal(
                barrier, inc=1, device_id=(row + dr, col + dc), device_id_type=MESH
            )

    def beside_count(pos, n):
        return jnp.where(pos > 0, 1, 0) + jnp.where(pos < n - 1, 1, 0)

    def meet():
        corners = beside_count(row, n_row) * beside_count(col, n_col)
        pl.semaphore_wait(barrier, n_row + n_col - 2 + corners)

    def message(k, i, receiving=False):
        dr, dc = STEPS[i]
        v = vecs[k]
        low, high = side_t.at[k, pl.ds(0, 8)], side_t.at[k, pl.ds(4 * rows - 8, 8)]
        src, dst = (
            (v.at[pl.ds(2, 2)], v.at[pl.ds(rows + 2, 2)]),
            (v.at[pl.ds(rows, 2)], v.at[pl.ds(0, 2)]),
            (side.at[k], from_right.at[k]),
            (side.at[k], from_left.at[k]),
            (high, corner.at[k, 0]),
            (high, corner.at[k, 1]),
            (low, corner.at[k, 2]),
            (low, corner.at[k, 3]),
        )[i]
        sign = -1 if receiving else 1
        return pltpu.make_async_remote_copy(
            src_ref=src, dst_ref=dst, send_sem=send_sem.at[k, i], recv_sem=recv_sem.at[k, i],
            device_id=(row + sign * dr, col + sign * dc), device_id_type=MESH,
        )

    def send(k, which):
        for i in which:
            @pl.when(exists(*STEPS[i]))
            def _():
                message(k, i).start()

    def receive(k, which):
        for i in which:
            dr, dc = STEPS[i]
            @pl.when(exists(-dr, -dc))
            def _():
                message(k, i, True).wait_recv()

    for i, (dr, dc) in enumerate(STEPS):
        @pl.when(jnp.logical_not(exists(-dr, -dc)))
        def _():
            for k in range(ITERS):
                if i == 0:
                    vecs[k][pl.ds(rows + 2, 2)] = jnp.zeros((2, ND, cols), jnp.float32)
                elif i == 1:
                    vecs[k][pl.ds(0, 2)] = jnp.zeros((2, ND, cols), jnp.float32)
                elif i == 2:
                    from_right[k] = jnp.zeros((ND, cols), jnp.float32)
                elif i == 3:
                    from_left[k] = jnp.zeros((ND, cols), jnp.float32)
                else:
                    corner[k, i - 4] = jnp.zeros((8, ND), jnp.float32)

    acc[...] = jnp.zeros_like(acc)
    lane = lax.broadcasted_iota(jnp.int32, (ND, cols), 1)

    dates = lax.broadcasted_iota(jnp.int32, (ND, count), 0)
    pull = (dates == pairs[1:2, :]).astype(jnp.float32) - (dates == pairs[0:1, :]).astype(
        jnp.float32
    )
    pull = pull.astype(jnp.bfloat16)
    gram = lax.dot_general(
        pull, pull, (((1,), (1,)), ((), ())), preferred_element_type=jnp.float32
    )
    gram_high, gram_low = split(gram)
    normal = jnp.concatenate(
        [
            jnp.concatenate([gram_high, gram_high], axis=1),
            jnp.concatenate([gram_low, gram_low], axis=1),
        ],
        axis=0,
    )

    shift = 2.0 * count / ND + 20.0 * LAM * LAM
    scale = 0.75 * shift
    k2 = LAM * LAM / scale

    def put(k, r, x0, x1):
        vecs[k][r + 2] = x0
        vecs[k][r + 3] = x1
        side[k] = jnp.where(
            lane // 4 == r,
            pltpu.roll(x0, 4 * r + 2, 1),
            jnp.where(lane // 4 == r + 1, pltpu.roll(x1, lax.rem(4 * r + 6, cols), 1), side[k]),
        )

    def pulled(t, p):
        flat = held.at[t].reshape(count * 8, cols)
        x = jnp.concatenate(
            [flat[pl.ds(2 * p + j, count, stride=8), :] for j in range(2)], axis=1
        )
        square = x * x
        acc[6] += folded(square[:, :cols] + square[:, cols:])
        high, low = split(x)
        b = jnp.dot(pull, high, preferred_element_type=jnp.float32) + jnp.dot(
            pull, low, preferred_element_type=jnp.float32
        )
        r = 8 * t + 2 * p
        put(0, r, b[:, :cols], b[:, cols:])

    side[0] = jnp.zeros((ND, cols), jnp.float32)
    for n, t in enumerate(order):
        loads[t].wait()

        @pl.loop(0, 4)
        def _(p):
            pulled(t, p)

        if n == min(1, tiles - 1):
            meet()
            send(0, (0, 1))

    def finish_sides(k):
        send(k, (2, 3))
        side_t[k] = side[k].T
        send(k, (4, 5, 6, 7))

    finish_sides(0)

    sub = lax.broadcasted_iota(jnp.int32, (cols, ND), 0)
    col_out = jnp.where(jnp.logical_and(lane == 0, col == 0), 1.0, 0.0) + jnp.where(
        jnp.logical_and(lane == cols - 1, col == n_col - 1), 1.0, 0.0
    )

    def horizontal(x, y):
        return pltpu.roll(jnp.where(lane == cols - 1, y, x), 1, 1) + pltpu.roll(
            jnp.where(lane == 0, y, x), cols - 1, 1
        )

    source = lax.broadcasted_iota(jnp.int32, (cols, 2 * cols), 0)
    target = lax.broadcasted_iota(jnp.int32, (cols, 2 * cols), 1)
    first = target < cols
    target = jnp.where(first, target, target - cols)

    def band(gap):
        near = jnp.where(gap == 1, jnp.where(first, 1.0, -8.0), 0.0)
        return near + jnp.where(
            first, 0.0, jnp.where(gap == 2, 1.0, jnp.where(gap == 0, 20.0, 0.0))
        )

    within = band(jnp.abs(source - target))
    outer = jnp.where(
        source >= cols - 2,
        band(jnp.abs(source - cols - target)),
        jnp.where(source < 2, band(jnp.abs(source + cols - target)), 0.0),
    )
    inner_bands = jnp.concatenate([within, within], axis=0).astype(jnp.bfloat16)
    outer_bands = jnp.concatenate([outer, outer], axis=0).astype(jnp.bfloat16)

    for k in range(ITERS):
        v = vecs[k]
        last = k == ITERS - 1

        @pl.loop(0, pairs_of_rows, unroll=4)
        def _(p):
            r = 2 * p
            x = jnp.concatenate([v[r + 2], v[r + 3]], axis=1)
            high, low = split(x)
            y = jnp.dot(
                normal, jnp.concatenate([high, low], axis=0), preferred_element_type=jnp.float32
            )
            y = (y[:ND] + y[ND:]) * (1.0 / scale)
            near = jnp.dot(
                jnp.concatenate(
                    [
                        jnp.concatenate([high[:, :cols], low[:, :cols]], axis=1),
                        jnp.concatenate([high[:, cols:], low[:, cols:]], axis=1),
                    ],
                    axis=0,
                ),
                inner_bands,
                preferred_element_type=jnp.float32,
            )
            for j in range(2):
                here = near[j * ND : (j + 1) * ND]
                beside[r + j + 1] = here[:, :cols]
                temp[r + j] = (
                    y[:, j * cols : (j + 1) * cols]
                    + k2 * here[:, cols:]
                    - (shift / scale + k2 * col_out) * x[:, j * cols : (j + 1) * cols]
                )

        for r, at_edge in ((0, row == 0), (rows - 1, row == n_row - 1)):
            @pl.when(at_edge)
            def _():
                temp[r] = temp[r] - k2 * v[r + 2]

        receive(k, (2, 3))
        side_in = jnp.where(lax.rem(lane, 4) < 2, from_left[k], from_right[k])

        group = 4

        @pl.loop(0, rows // group, unroll=2)
        def _(g):
            start = group * g
            lhs = []
            for j in range(group):
                y = pltpu.roll(side_in, lax.rem(2 * cols - 2 - 4 * (start + j), cols), 1)
                lhs.append(jnp.concatenate(split(y), axis=1))
            both = jnp.dot(
                jnp.concatenate(lhs, axis=0), outer_bands, preferred_element_type=jnp.float32
            )
            for j in range(group):
                r = start + j
                got = both[j * ND : (j + 1) * ND]
                beside[r + 1] += got[:, :cols]
                temp[r] += k2 * got[:, cols:]

        receive(k, (0, 1, 4, 5, 6, 7))
        for at, h_at, left, right, a, b in (
            (1, 0, 0, 1, 5, 6),
            (rows + 2, rows + 1, 2, 3, 1, 2),
        ):
            m = jnp.where(
                sub == cols - 1,
                corner[k, left, pl.ds(a, 1), :],
                jnp.where(sub == 0, corner[k, right, pl.ds(b, 1), :], 0.0),
            )
            beside[h_at] = horizontal(v[at], m.T)

        if not last:
            side[k + 1] = jnp.zeros((ND, cols), jnp.float32)

        def both_rows(p):
            r = 2 * p
            x = [v[r + j] for j in range(6)]
            h = [beside[r + j] for j in range(4)]
            new = [
                temp[r + j]
                + k2 * (2.0 * (h[j] + h[j + 2]) + (x[j] + x[j + 4]) - 8.0 * (x[j + 1] + x[j + 3]))
                for j in range(2)
            ]
            if k == 0:
                acc[0] += folded(x[2] * x[2] + x[3] * x[3])
            acc[2 * k + 1] += folded(x[2] * new[0] + x[3] * new[1])
            if not last:
                acc[2 * k + 2] += folded(new[0] * new[0] + new[1] * new[1])
                put(k + 1, r, new[0], new[1])

        @pl.loop(0, 2)
        def _(e):
            both_rows(e * (pairs_of_rows - 1))

        if not last:
            send(k + 1, (0, 1))

        @pl.loop(1, pairs_of_rows - 1, unroll=2)
        def _(p):
            both_rows(p)

        if not last:
            finish_sides(k + 1)

    slot = lax.broadcasted_iota(jnp.int32, (8, cols), 0)
    local = jnp.zeros((8, cols), jnp.float32)
    for j in range(7):
        local = jnp.where(slot == j, jnp.sum(acc[j], axis=0, keepdims=True), local)

    def gather(source, into, send_s, recv_s, me, n, where_to):
        into[me] = source[...]
        copies = []
        for d in range(1, n):
            c = pltpu.make_async_remote_copy(
                src_ref=source, dst_ref=into.at[n + d], send_sem=send_s.at[d],
                recv_sem=recv_s.at[d], device_id=where_to(lax.rem(me + d, n)),
                device_id_type=MESH,
            )
            c.start()
            copies.append(c)
        for d, c in enumerate(copies, 1):
            c.wait()
            into[lax.rem(me + n - d, n)] = into[n + d]
        total = into[0]
        for i in range(1, n):
            total = total + into[i]
        return total

    mine[...] = local
    part[...] = gather(mine, cols_in, col_send, col_recv, col, n_col, lambda c: (row, c))
    sums = gather(part, rows_in, row_send, row_recv, row, n_row, lambda r: (r, col))
    sums = jnp.broadcast_to(jnp.sum(sums, axis=1, keepdims=True), (8, cols))
    mu = [sums[j : j + 1] for j in range(6)]
    y = coefficients(mu, jnp.sqrt(sums[6:7]), shift, scale)

    @pl.loop(0, rows, unroll=4)
    def _(r):
        out[pl.ds(r, ND, stride=rows), :] = y[0] * v0[r + 2] + y[1] * v1[r + 2] + y[2] * v2[r + 2]

    for k in range(ITERS):
        for i, step in enumerate(STEPS):
            @pl.when(exists(*step))
            def _():
                message(k, i).wait_send()


def on_device(n_row, n_col, phase, pairs):
    count, rows, cols = phase.shape
    assert rows % 8 == 0 and 4 * rows == cols and cols == ND
    f32 = jnp.float32
    dma = pltpu.SemaphoreType.DMA
    result = pl.pallas_call(
        functools.partial(kernel, (n_row, n_col, count, rows, cols)),
        out_shape=jax.ShapeDtypeStruct((ND * rows, cols), f32),
        in_specs=[pl.BlockSpec(memory_space=pl.ANY), pl.BlockSpec(memory_space=pltpu.VMEM)],
        out_specs=pl.BlockSpec(memory_space=pltpu.VMEM),
        scratch_shapes=[
            pltpu.VMEM((rows // 8, count, 8, cols), f32),
            pltpu.VMEM((rows + 4, ND, cols), f32),
            pltpu.VMEM((rows + 4, ND, cols), f32),
            pltpu.VMEM((rows + 4, ND, cols), f32),
            pltpu.VMEM((ITERS, ND, cols), f32),
            pltpu.VMEM((ITERS, cols, ND), f32),
            pltpu.VMEM((ITERS, ND, cols), f32),
            pltpu.VMEM((ITERS, ND, cols), f32),
            pltpu.VMEM((ITERS, 4, 8, ND), f32),
            pltpu.VMEM((rows + 2, ND, cols), f32),
            pltpu.VMEM((rows, ND, cols), f32),
            pltpu.VMEM((8, 8, cols), f32),
            pltpu.VMEM((8, cols), f32),
            pltpu.VMEM((2 * n_col, 8, cols), f32),
            pltpu.VMEM((8, cols), f32),
            pltpu.VMEM((2 * n_row, 8, cols), f32),
            dma((rows // 8,)),
            dma((ITERS, 8)),
            dma((ITERS, 8)),
            dma((n_col,)),
            dma((n_col,)),
            dma((n_row,)),
            dma((n_row,)),
        ],
        compiler_params=pltpu.CompilerParams(
            collective_id=0, has_side_effects=True, vmem_limit_bytes=48 * 1024 * 1024
        ),
    )(phase.reshape(count, rows // 8, 8, cols), pairs.T)
    return result.reshape(ND, rows, cols)


def solution(mesh):
    shape = mesh.shape
    return jax.shard_map(
        functools.partial(on_device, shape["row"], shape["col"]),
        mesh=mesh,
        in_specs=(P(None, "row", "col"), P()),
        out_specs=P(None, "row", "col"),
        check_vma=False,
    )
```
